32 devices in a mesh: ctx: 4 (over y, x), exp: 8 (over z, core).
Axes of the slice: x: 2, y: 2, z: 4, core: 2. Of those that a mesh axis runs over, the one named last changes fastest.
Arguments:
- queries: bfloat16 [8, 512, 4096], P('exp', 'ctx'), may hold values from -48 to 48
- keys: bfloat16 [8, 512, 256], P('exp', 'ctx'), may hold values from -4 to 4
- values: bfloat16 [8, 512, 256], P('exp', 'ctx'), may hold values from -6 to 6
- positions: int32 [8, 512], P('exp', 'ctx'), may hold values from 0 to 65535, as said below
- residual: bfloat16 [8, 512, 4096], P('exp', 'ctx'), may hold values from -6 to 6
- norm_gain: float32 [4096], replicated, may hold values from 0.25 to 1.75
- expert_ids: int32 [8, 512, 8], P('exp', 'ctx'), may hold values from 0 to 127, as said below
- route_weights: float32 [8, 512, 8], P('exp', 'ctx'), may hold values from 0.3 to 1
- w_gate: bfloat16 [8, 4096, 1536], P('exp', None, 'ctx'), may hold values from -0.09375 to 0.09375
- w_up: bfloat16 [8, 4096, 1536], P('exp', None, 'ctx'), may hold values from -0.09375 to 0.09375
- w_down: bfloat16 [8, 1536, 4096], P('exp', None, 'ctx'), may hold values from -0.15625 to 0.15625
Outputs:
- layer_out: bfloat16 [8, 512, 4096], P('exp', 'ctx')
The draws below stay inside these ranges and needn't reach their ends.
Inputs may be any that keep to these rules, and one draw needn't show every extreme that they name: `positions`: strictly increasing along each sequence. `expert_ids`: A token's 8 ids differ. In each aligned block of 128 tokens of a sequence no id is named by more than 9 tokens.
All inputs are finite; a program needn't handle non-finite values.
Results may differ from the reference program's by a relative error of at most 0.007.
Values may be sent and summed in bfloat16 or wider, within the bound.
A program may use at most 128 MiB of HBM per device.

```python
import math
import jax
import jax.numpy as jnp
from jax import lax

D = 4096
HEADS = 32
KV_HEADS = 2
HEAD_DIM = 128
FF = 1536
ROUTED = 128
TOP = 8
TOK_DEV = 128
EXPERTS = 8
LENGTH = 512
SEQS = 8
CAP = 9
N_CTX = 4


def base_keys(key):
    raw = jax.random.normal(jax.random.fold_in(key, 11), (SEQS, LENGTH, KV_HEADS * HEAD_DIM), jnp.float32)
    return jnp.clip(raw, -4.0, 4.0)


def draw_keys(key, part):
    return base_keys(key).astype(jnp.bfloat16)


def draw_queries(key, part):
    raw = jax.random.normal(jax.random.fold_in(key, 12), (SEQS, LENGTH, HEADS * HEAD_DIM), jnp.float32)
    result = jnp.clip(raw, -5.0, 5.0)
    return result.astype(jnp.bfloat16)


def draw_positions(key, part):
    gaps = jax.random.randint(jax.random.fold_in(key, 21), (SEQS, LENGTH), 1, 3, dtype=jnp.int32)
    ends = jax.random.randint(jax.random.fold_in(key, 22), (SEQS, 1), 2 * LENGTH, 65536, dtype=jnp.int32)
    ends = ends.at[0, 0].set(65535)
    running = jnp.cumsum(gaps, axis=1).astype(jnp.int32)
    return (ends - running[:, -1:] + running).astype(jnp.int32)


def draw_expert_ids(key, part):
    blocks = SEQS * LENGTH // TOK_DEV
    mean_count = TOK_DEV * TOP // ROUTED
    full_expert = jax.random.randint(jax.random.fold_in(key, 31), (), 0, EXPERTS, dtype=jnp.int32)
    block_keys = jax.random.split(jax.random.fold_in(key, 32), blocks)

    def one_block(block_key):
        key_order, key_signs, key_runs, key_tokens = jax.random.split(block_key, 4)
        order = jax.random.permutation(key_order, ROUTED).astype(jnp.int32)
        where_full = jnp.argmax(order == full_expert)
        leading = order[0]
        order = order.at[where_full].set(leading).at[0].set(full_expert)
        signs = jax.random.randint(key_signs, (ROUTED,), 0, 2, dtype=jnp.int32)
        signs = signs.at[0].set(1).at[ROUTED - 1].set(0)
        change = signs - jnp.roll(signs, 1)
        counts = (mean_count + jnp.zeros((ROUTED,), jnp.int32).at[order].set(change)).astype(jnp.int32)
        runs = jax.random.permutation(key_runs, ROUTED).astype(jnp.int32)
        ends = jnp.cumsum(counts[runs]).astype(jnp.int32)
        places = jnp.arange(TOK_DEV * TOP, dtype=jnp.int32)
        which = jnp.sum((places[:, None] >= ends[None, :]).astype(jnp.int32), axis=1)
        expert_at = runs[which]
        table = expert_at.reshape(TOP, TOK_DEV).T
        shuffle = jax.random.permutation(key_tokens, TOK_DEV).astype(jnp.int32)
        return table[shuffle]
    chosen = jax.vmap(one_block)(block_keys)
    return chosen.reshape(SEQS, LENGTH, TOP).astype(jnp.int32)


def levels(rng, dims, cuts, least, high):
    factor_of = 1.0
    for position, parts in cuts:
        steps = jax.random.uniform(jax.random.fold_in(jax.random.fold_in(rng, 6), position), (parts,), jnp.float32, least / len(cuts), high / len(cuts))
        factor_of = factor_of * jnp.repeat(jnp.exp(steps), dims[position] // parts).reshape((-1,) + (1,) * (len(dims) - 1 - position))
    return factor_of


def centred(key, dims, scale, bound, cuts=(), kind=jnp.bfloat16):
    values = scale * jax.random.normal(key, dims, jnp.float32)
    if cuts:
        values = values * levels(key, dims, cuts, -0.22, 0.18)
    return jnp.clip(values, -bound, bound).astype(kind)


def setup_inputs(seed: int = 0) -> dict:
    arg_keys = jax.random.split(jax.random.key(seed), 12)
    return {
        "queries": draw_queries(jax.random.fold_in(arg_keys[11], 71), 0),
        "keys": draw_keys(jax.random.fold_in(arg_keys[11], 71), 0),
        "values": centred(arg_keys[2], (SEQS, LENGTH, KV_HEADS * HEAD_DIM), 1.0, 6.0, ((0, 8), (1, 4))),
        "positions": draw_positions(jax.random.fold_in(arg_keys[11], 71), 0),
        "residual": centred(arg_keys[4], (SEQS, LENGTH, D), 1.0, 6.0, ((0, 8), (1, 4))),
        "norm_gain": jnp.clip(1.0 + 0.15 * jax.random.normal(arg_keys[5], (D,), jnp.float32), 0.25, 1.75),
        "expert_ids": draw_expert_ids(jax.random.fold_in(arg_keys[11], 71), 0),
        "route_weights": jnp.clip(0.3 + 0.7 * jax.random.uniform(arg_keys[7], (SEQS, LENGTH, TOP), jnp.float32) ** levels(arg_keys[7], (SEQS, LENGTH, TOP), ((0, 8), (1, 4)), -0.2, 0.2), 0.3, 1.0),
        "w_gate": centred(arg_keys[8], (EXPERTS, D, FF), D ** -0.5, 0.09375, ((0, 8), (2, 4))),
        "w_up": centred(arg_keys[9], (EXPERTS, D, FF), D ** -0.5, 0.09375, ((0, 8), (2, 4))),
        "w_down": centred(arg_keys[10], (EXPERTS, FF, D), FF ** -0.5, 0.15625, ((0, 8), (2, 4))),
    }


def yarn_tables(position_values):
    half = HEAD_DIM // 2
    theta_base = 1000000.0
    factor = 4.0
    trained_span = 32768.0

    def bound_dim(turns):
        return HEAD_DIM * math.log(trained_span / (turns * 2 * math.pi)) / (2 * math.log(theta_base))
    lower = max(math.floor(bound_dim(32.0)), 0)
    upper = min(math.ceil(bound_dim(1.0)), HEAD_DIM - 1)
    pair_index = jnp.arange(half, dtype=jnp.float32)
    extrapolated = jnp.exp(-(2.0 * pair_index / HEAD_DIM) * math.log(theta_base))
    ramp = jnp.clip((pair_index - lower) / max(upper - lower, 1), 0.0, 1.0)
    inverse = extrapolated / factor * ramp + extrapolated * (1.0 - ramp)
    magnitude = 0.1 * math.log(factor) + 1.0
    angles = position_values.astype(jnp.float32)[..., None] * inverse
    return (jnp.cos(angles) * magnitude, jnp.sin(angles) * magnitude)

def rotate_heads(field, cosine, sine):
    half = HEAD_DIM // 2
    first = field[..., :half]
    second = field[..., half:]
    return jnp.concatenate([first * cosine - second * sine, second * cosine + first * sine], axis=-1)

def attend_sequence(inputs):
    query_rows, key_rows, value_rows, position_row = inputs
    length = query_rows.shape[0]
    group = HEADS // KV_HEADS
    cosine, sine = yarn_tables(position_row)
    cosine = cosine[:, None, :]
    sine = sine[:, None, :]
    q_rot = rotate_heads(query_rows.reshape(length, HEADS, HEAD_DIM).astype(jnp.float32), cosine, sine).astype(jnp.bfloat16)
    k_rot = rotate_heads(key_rows.reshape(length, KV_HEADS, HEAD_DIM).astype(jnp.float32), cosine, sine).astype(jnp.bfloat16)
    grouped = q_rot.reshape(length, KV_HEADS, group, HEAD_DIM).astype(jnp.float32)
    scores = jnp.einsum('tkgd,nkd->kgtn', grouped, k_rot.astype(jnp.float32)) / math.sqrt(HEAD_DIM)
    allowed = position_row[None, :] <= position_row[:, None]
    scores = jnp.where(allowed, scores, jnp.float32(-1e+30))
    largest = lax.optimization_barrier(jnp.max(scores, axis=-1, keepdims=True))
    weight = jnp.where(allowed, jnp.exp(scores - largest), jnp.float32(0.0))
    total = lax.optimization_barrier(jnp.sum(weight, axis=-1))
    weight_b = weight.astype(jnp.bfloat16).astype(jnp.float32)
    value_heads = value_rows.reshape(length, KV_HEADS, HEAD_DIM).astype(jnp.float32)
    mixed = jnp.einsum('kgtn,nkd->kgtd', weight_b, value_heads) / total[..., None]
    return jnp.transpose(mixed, (2, 0, 1, 3)).reshape(length, HEADS * HEAD_DIM)

def reference(queries, keys, values, positions, residual, norm_gain, expert_ids, route_weights, w_gate, w_up, w_down):
    seq_count, length, width = queries.shape
    attn = lax.map(attend_sequence, (queries, keys, values, positions))
    h_state = residual.astype(jnp.float32) + attn
    mean_square = lax.optimization_barrier(jnp.mean(h_state * h_state, axis=-1, keepdims=True))
    normed = (h_state / jnp.sqrt(mean_square + 1e-06) * norm_gain).astype(jnp.bfloat16)
    flat_rows = normed.reshape(seq_count * length, width)
    flat_ids = expert_ids.reshape(-1)
    flat_weights = route_weights.reshape(-1)
    assignments = flat_ids.shape[0]
    most_rows = seq_count * N_CTX * CAP
    choice_index = jnp.arange(assignments, dtype=jnp.int32)

    def add_expert(expert, total):
        chosen = flat_ids == expert
        rank = jnp.cumsum(chosen.astype(jnp.int32)).astype(jnp.int32) - 1
        target = jnp.where(chosen, rank, most_rows).astype(jnp.int32)
        owner = jnp.zeros((most_rows,), jnp.int32).at[target].set(choice_index, mode='drop')
        filled = jnp.zeros((most_rows,), jnp.float32).at[target].set(1.0, mode='drop')
        token_index = (owner // TOP).astype(jnp.int32)
        rows = flat_rows[token_index]
        gate = jnp.dot(rows, w_gate[expert], preferred_element_type=jnp.float32)
        upper = jnp.dot(rows, w_up[expert], preferred_element_type=jnp.float32)
        act = (jax.nn.silu(gate) * upper).astype(jnp.bfloat16)
        out_rows = jnp.dot(act, w_down[expert], preferred_element_type=jnp.float32).astype(jnp.bfloat16)
        scaled = out_rows.astype(jnp.float32) * (flat_weights[owner] * filled)[:, None]
        return total.at[token_index].add(scaled)
    moe_sum = lax.fori_loop(0, EXPERTS, add_expert, jnp.zeros((seq_count * length, width), jnp.float32))
    layer_out = h_state + moe_sum.reshape(seq_count, length, width)
    return layer_out.astype(jnp.bfloat16)
```

```python
import functools
import heapq
import math

import jax
import jax.numpy as jnp
from jax import lax
from jax.experimental import pallas as pl
from jax.experimental.pallas import tpu as pltpu
from jax.sharding import PartitionSpec as P

HEADS = 32
KV_HEADS = 2
HEAD_DIM = 128
ROUTED = 128
TOP = 8
PIECES = 4
HOLD = 11.0
MESH = pl.DeviceIdType.MESH
F32 = jnp.float32
BF16 = jnp.bfloat16


def yarn_frequencies():
    half = HEAD_DIM // 2
    theta_base = 1000000.0
    factor = 4.0
    trained_span = 32768.0

    def bound_dim(turns):
        return (
            HEAD_DIM * math.log(trained_span / (turns * 2 * math.pi)) / (2 * math.log(theta_base))
        )

    lower = max(math.floor(bound_dim(32.0)), 0)
    upper = min(math.ceil(bound_dim(1.0)), HEAD_DIM - 1)
    pair_index = jnp.arange(half, dtype=jnp.float32)
    extrapolated = jnp.exp(-(2.0 * pair_index / HEAD_DIM) * math.log(theta_base))
    ramp = jnp.clip((pair_index - lower) / max(upper - lower, 1), 0.0, 1.0)
    return extrapolated / factor * ramp + extrapolated * (1.0 - ramp)


def flip(index, offset, count):
    bit = 1
    out = index
    while bit < count:
        if offset & bit:
            out = out + bit - 2 * bit * lax.rem(lax.div(index, bit), 2)
        bit *= 2
    return out


def plan(n_k, n_pieces):
    gap, hop, far = 1.5, 1.4, n_pieces - 1
    heap = []
    for k in range(n_k):
        heapq.heappush(heap, (gap * k, 0, k, "send"))
        heapq.heappush(heap, (gap * n_k - 1.4, 1 + k, k, "far"))
        heapq.heappush(heap, (gap * k + hop, 0, k, "spread"))
        for i in range(1, far):
            start = 3.6 if i == far - 1 else 6.0
            heapq.heappush(heap, (gap * k + start, i, k, "spread"))
        heapq.heappush(heap, (gap * n_k + 3.0 + 1.5 * k, far, k, "spread"))
    link = 0.0
    left = [n_k] * n_pieces
    events = []
    while heap:
        at, i, k, kind = heapq.heappop(heap)
        events.append((kind, i, k))
        if kind == "spread":
            link = max(link, at) + 0.73
            heapq.heappush(heap, (max(link + hop, 0 if i else HOLD), i, k, "relay"))
        elif kind == "relay":
            link = max(link, at) + 0.37
            heapq.heappush(heap, (link + hop, i, k, "gate_up"))
        elif kind == "gate_up":
            left[i] -= 1
            if not left[i]:
                link = max(link, at) + 2.0
                heapq.heappush(heap, (link + hop, i, n_k, "down"))
        elif kind == "down":
            link = max(link, at) + 1.5
    return events


def dot(a, b):
    return jnp.dot(a, b, preferred_element_type=F32)


def kernel(
    n_ctx,
    n_exp,
    q_hbm,
    k_hbm,
    v_hbm,
    pos_hbm,
    inv_hbm,
    res_hbm,
    gain_hbm,
    ids_hbm,
    rw_hbm,
    wg_hbm,
    wu_hbm,
    wd_hbm,
    out_ref,
    q_ref,
    k_ref,
    pos_ref,
    inv_ref,
    gain_ref,
    ids_ref,
    rw_ref,
    res_ref,
    kv,
    hst,
    sqr,
    disp,
    hid,
    xbuf,
    gacc,
    uacc,
    act,
    obuf,
    ret,
    mix,
    wg,
    wu,
    wd,
    w_sem,
    kv_send,
    kv_recv,
    z_send,
    z_recv,
    xy_send,
    xy_recv,
    act_send,
    act_recv,
    ret_send,
    ret_recv,
):
    my_c = lax.axis_index("ctx")
    my_e = lax.axis_index("exp")
    tokens, width = q_hbm.shape[1:]
    fold = tokens * TOP // ROUTED
    slots = n_exp * fold
    hidden = wd.shape[0] // n_ctx
    cols = wd.shape[1]
    cpart = cols // fold
    n_chunks = PIECES
    chunk = n_exp // n_chunks
    wide = fold * HEAD_DIM
    n_k = width // wide
    step_cols = wide + HEAD_DIM
    group = HEADS // KV_HEADS
    paired = hidden % 128 == 0
    gate_dst = wg.at[:, :hidden] if paired else wg
    up_dst = wg.at[:, hidden:] if paired else wu

    barrier = pltpu.get_barrier_semaphore()
    for m in range(1, n_ctx):
        pl.semaphore_signal(
            barrier, inc=1, device_id=(flip(my_c, m, n_ctx), my_e), device_id_type=MESH
        )
    for d in range(1, n_exp):
        pl.semaphore_signal(
            barrier, inc=1, device_id=(my_c, flip(my_e, d, n_exp)), device_id_type=MESH
        )

    def load(i, src, dst):
        return pltpu.make_async_copy(src, dst, w_sem.at[i])

    small = [
        load(i, src, dst)
        for i, (src, dst) in enumerate(
            (
                (pos_hbm, pos_ref),
                (inv_hbm, inv_ref),
                (k_hbm, k_ref),
                (ids_hbm, ids_ref),
                (rw_hbm, rw_ref),
                (gain_hbm, gain_ref),
            )
        )
    ]
    values = [
        load(6 + g, v_hbm.at[:, g * HEAD_DIM : (g + 1) * HEAD_DIM], kv.at[my_c, g, 1])
        for g in range(KV_HEADS)
    ]
    loads = [
        load(6 + KV_HEADS + i, src.at[0], dst)
        for i, (src, dst) in enumerate(
            ((q_hbm, q_ref), (res_hbm, res_ref), (wg_hbm, gate_dst), (wu_hbm, up_dst), (wd_hbm, wd))
        )
    ]
    for copy in small + values + loads:
        copy.start()

    for copy in small[:2]:
        copy.wait()
    angles = jnp.broadcast_to(pos_ref[...].astype(F32), (HEAD_DIM, tokens)).T * inv_ref[...]
    magnitude = 0.1 * math.log(4.0) + 1.0
    cosine = jnp.cos(angles) * magnitude
    sine = jnp.sin(angles) * magnitude
    side = lax.broadcasted_iota(jnp.int32, (tokens, HEAD_DIM), 1)
    sine = jnp.where(side < HEAD_DIM // 2, -sine, sine)
    for copy in small[2:] + values:
        copy.wait()

    def rotate(x):
        return (x * cosine + pltpu.roll(x, HEAD_DIM // 2, 1) * sine).astype(BF16)

    for g in range(KV_HEADS):
        lanes = slice(g * HEAD_DIM, (g + 1) * HEAD_DIM)
        kv[my_c, g, 0] = rotate(k_ref[:, lanes].astype(F32))

    pl.semaphore_wait(barrier, n_ctx + n_exp - 2)

    def kv_copy(g, m):
        return pltpu.make_async_remote_copy(
            src_ref=kv.at[my_c, g],
            dst_ref=kv.at[my_c, g],
            send_sem=kv_send.at[g, m],
            recv_sem=kv_recv.at[g, m],
            device_id=(flip(my_c, m, n_ctx), my_e),
            device_id_type=MESH,
        )

    for g in range(KV_HEADS):
        for m in range(1, n_ctx):

            @pl.when(flip(my_c, m, n_ctx) > my_c)
            def _():
                kv_copy(g, m).start()

    loads[0].wait()
    for h in range(HEADS):
        at = slice(h * HEAD_DIM, (h + 1) * HEAD_DIM)
        q_ref[:, at] = rotate(q_ref[:, at].astype(F32))

    slot = lax.broadcasted_iota(jnp.int32, (slots, tokens), 0)
    slot_off = slot // fold
    slot_rank = slot % fold
    expert_of = jnp.zeros((slots, tokens), jnp.int32)
    for d in range(n_exp):
        expert_of = jnp.where(slot_off == d, flip(my_e, d, n_exp), expert_of)
    named = jnp.zeros((slots, tokens), F32)
    weight = jnp.zeros((slots, tokens), F32)
    for k in range(TOP):
        hit = ids_ref[k : k + 1, :] == expert_of
        named = named + jnp.where(hit, 1.0, 0.0)
        weight = weight + jnp.where(hit, rw_ref[k : k + 1, :], 0.0)
    row = lax.broadcasted_iota(jnp.int32, (tokens, tokens), 0)
    col = lax.broadcasted_iota(jnp.int32, (tokens, tokens), 1)
    earlier = jnp.where(row < col, 1.0, 0.0).astype(BF16)
    rank = dot(named.astype(BF16), earlier)
    sel_main = jnp.where(rank == slot_rank.astype(F32), named, 0.0)
    sel_last = jnp.where(rank == float(fold), named, 0.0)
    both_t = jnp.concatenate([sel_main, sel_last], axis=0).astype(BF16)
    rank_lane = lax.broadcasted_iota(jnp.int32, (slots, HEAD_DIM), 0) % fold
    for i, sel in enumerate((sel_main, sel_last)):
        both = jnp.where(sel > 0.5, weight, 0.0).T
        high = both.astype(BF16)
        mix[i, :, :slots] = high
        mix[i, :, slots:] = (both - high.astype(F32)).astype(BF16)

    inv_root = 1.0 / math.sqrt(HEAD_DIM)
    to_two = inv_root / math.log(2.0)
    loads[1].wait()

    def attend(first, count):
        g = first // group
        for c in range(n_ctx):

            @pl.when(my_c == c)
            def _():
                if first % group == 0:
                    for other in range(c):
                        kv_copy(g, c ^ other).wait_recv()
                length = (c + 1) * tokens
                key_head = kv[: c + 1, g, 0].reshape(length, HEAD_DIM)
                value_head = kv[: c + 1, g, 1].reshape(length, HEAD_DIM)
                value_head = jnp.concatenate([value_head, jnp.ones_like(value_head)], axis=1)
                q_row = lax.broadcasted_iota(jnp.int32, (tokens, tokens), 0)
                k_col = lax.broadcasted_iota(jnp.int32, (tokens, tokens), 1)

                def head(h):
                    at = pl.ds(pl.multiple_of(h * HEAD_DIM, HEAD_DIM), HEAD_DIM)
                    scores = lax.dot_general(
                        q_ref[:, at],
                        key_head,
                        (((1,), (1,)), ((), ())),
                        preferred_element_type=F32,
                    )
                    own = jnp.where(k_col <= q_row, scores[:, c * tokens :], -1e30)
                    if c:
                        scores = jnp.concatenate([scores[:, : c * tokens], own], axis=1)
                    else:
                        scores = own
                    top = jnp.max(scores, axis=-1, keepdims=True)
                    p = jnp.exp2((scores - top) * to_two).astype(BF16)
                    mixed = dot(p, value_head)
                    attn = mixed[:, :HEAD_DIM] / mixed[:, HEAD_DIM:]
                    hidden_row = res_ref[:, at].astype(F32) + attn
                    hst[:, at] = hidden_row
                    return hidden_row * hidden_row

                unroll = min(count, 4) if n_ctx <= 4 else 1
                square = jnp.zeros((tokens, HEAD_DIM), F32)
                if unroll == count:
                    for u in range(count):
                        square = square + head(first + u)
                else:

                    def several(i, square):
                        for u in range(unroll):
                            square = square + head(first + i * unroll + u)
                        return square

                    square = lax.fori_loop(0, count // unroll, several, square)
                if first:
                    sqr[...] += square
                else:
                    sqr[...] = square

    def chunk_at(k):
        return slice(k * step_cols, (k + 1) * step_cols + (HEAD_DIM if k == n_k - 1 else 0))

    def z_copy(k, d):
        return pltpu.make_async_remote_copy(
            src_ref=disp.at[d, :, chunk_at(k)],
            dst_ref=hid.at[my_c, d, :, chunk_at(k)],
            send_sem=z_send.at[k, d],
            recv_sem=z_recv.at[k, d],
            device_id=(my_c, flip(my_e, d, n_exp)),
            device_id_type=MESH,
        )

    def xy_copy(m, k, d):
        return pltpu.make_async_remote_copy(
            src_ref=hid.at[my_c, d, :, chunk_at(k)],
            dst_ref=hid.at[my_c, d, :, chunk_at(k)],
            send_sem=xy_send.at[m, k, d],
            recv_sem=xy_recv.at[m, k, d],
            device_id=(flip(my_c, m, n_ctx), my_e),
            device_id_type=MESH,
        )

    def relay_copy(k, d):
        via = 1 + d % 2
        origin = flip(my_c, via, n_ctx)
        return pltpu.make_async_remote_copy(
            src_ref=hid.at[origin, d, :, chunk_at(k)],
            dst_ref=hid.at[origin, d, :, chunk_at(k)],
            send_sem=xy_send.at[3, k, d],
            recv_sem=xy_recv.at[3, k, d],
            device_id=(flip(my_c, 3 - via, n_ctx), my_e),
            device_id_type=MESH,
        )

    relayed = n_ctx == 4
    direct = (1, 2) if relayed else tuple(range(1, n_ctx))
    order = [[c * chunk + i for i in range(chunk)] for c in range(n_chunks)]

    def spread(k, ds):
        for d in ds:
            if d:
                z_copy(k, d).wait_recv()
            for m in direct:
                xy_copy(m, k, d).start()

    def relay(k, ds):
        if relayed:
            for d in ds:
                xy_copy(1 + d % 2, k, d).wait_recv()
                relay_copy(k, d).start()

    def put(at, value):
        value = value.reshape(n_exp, fold, value.shape[-1]).astype(BF16)
        disp[:, :, at] = value
        hid[my_c, 0, :, at] = value[0]

    def dispatch(k):
        base = k * step_cols
        rows = slice(k * wide, (k + 1) * wide)
        x = (hst[:, rows] * gain_ref[:, rows]).astype(BF16)
        picked = dot(both_t, x)
        put(slice(base, base + wide), picked[:slots])
        folded = picked[slots:, :HEAD_DIM]
        for j in range(1, fold):
            piece = picked[slots:, j * HEAD_DIM : (j + 1) * HEAD_DIM]
            folded = jnp.where(rank_lane == j, piece, folded)
        put(slice(base + wide, base + step_cols), folded)
        if k == n_k - 1:
            mean_square = jnp.sum(sqr[...], axis=-1, keepdims=True) * (1.0 / width)
            scale = 1.0 / jnp.sqrt(mean_square + 1e-06)
            scale = jnp.broadcast_to(scale, (tokens, HEAD_DIM))
            high = scale.astype(BF16)
            low = (scale - high.astype(F32)).astype(BF16)
            lane = lax.broadcasted_iota(jnp.int32, (tokens, HEAD_DIM), 1)
            pair = jnp.where(lane % 64 < 32, high, low)
            lane = lax.broadcasted_iota(jnp.int32, (slots, HEAD_DIM), 1)
            picked = dot(both_t, pair)
            picked = jnp.where(lane < 64, picked[:slots], picked[slots:])
            put(slice(base + step_cols, base + step_cols + HEAD_DIM), picked)
        for piece in reversed(order[:-1]):
            for d in piece:
                if d:
                    z_copy(k, d).start()
        spread(k, [0])

    def act_copy(m, i):
        return pltpu.make_async_remote_copy(
            src_ref=act.at[my_c, i],
            dst_ref=act.at[my_c, i],
            send_sem=act_send.at[m, i],
            recv_sem=act_recv.at[m, i],
            device_id=(flip(my_c, m, n_ctx), my_e),
            device_id_type=MESH,
        )

    def ret_copy(m, d):
        there = flip(my_c, m, n_ctx)
        return pltpu.make_async_remote_copy(
            src_ref=obuf.at[there, d],
            dst_ref=ret.at[my_c, d],
            send_sem=ret_send.at[m, d],
            recv_sem=ret_recv.at[m, d],
            device_id=(there, flip(my_e, d, n_exp)),
            device_id_type=MESH,
        )

    blocks = n_ctx * chunk
    body = blocks * fold
    pick_r = lax.broadcasted_iota(jnp.int32, (body, body), 0)
    pick_c = lax.broadcasted_iota(jnp.int32, (body, body), 1)
    pick_all = jnp.where(pick_c == pick_r % blocks * fold + pick_r // blocks, 1.0, 0.0)
    pick_all = pick_all.astype(BF16)
    gather_r = lax.broadcasted_iota(jnp.int32, (body, blocks), 0)
    gather_c = lax.broadcasted_iota(jnp.int32, (body, blocks), 1)
    tile = 256 if cols % 256 == 0 else cols

    def landed(i, lo, hi):
        ds = slice(order[i][0], order[i][0] + chunk)
        return hid[:, ds, :, lo:hi].astype(F32).reshape(body, hi - lo).astype(BF16)

    def gate_up(i, k, opening, first):
        for d in order[i]:
            if relayed:
                xy_copy(2 - d % 2, k, d).wait_recv()
                relay_copy(k, d).wait_recv()
            else:
                for m in direct:
                    xy_copy(m, k, d).wait_recv()
        if first:
            for copy in loads[2:]:
                copy.wait()
        base = k * step_cols
        xbuf[:body] = landed(i, base, base + wide)
        tails = dot(pick_all, landed(i, base + wide, base + step_cols)).astype(BF16)
        for j in range(fold):
            at = slice(j * HEAD_DIM, (j + 1) * HEAD_DIM)
            xbuf[body:, at] = tails[j * blocks : (j + 1) * blocks]
        for acc, weights in ((gacc, wg),) if paired else ((gacc, wg), (uacc, wu)):
            part = dot(xbuf[...], weights[k * wide : (k + 1) * wide])
            acc[i] = part if opening else acc[i] + part

    def activate(i):
        base = n_k * step_cols
        pair = landed(i, base, base + HEAD_DIM)
        first = dot(pick_all[:blocks], pair)
        pair = pair.astype(F32)
        scale = jnp.concatenate(
            [pair[:, :1] + pair[:, 32:33], first[:, 64:65] + first[:, 96:97]], axis=0
        )
        gate = gacc[i, :, :hidden] * scale
        upper = (gacc[i, :, hidden:] if paired else uacc[i]) * scale
        act[my_c, i] = (gate / (1.0 + jnp.exp(-gate)) * upper).astype(BF16)
        for m in range(1, n_ctx):
            act_copy(m, i).start()

    def down(i):
        ds = slice(order[i][0], order[i][0] + chunk)
        for m in range(1, n_ctx):
            act_copy(m, i).wait_recv()
        for t in range(cols // tile):
            at = slice(t * tile, (t + 1) * tile)
            y = jnp.zeros((body + blocks, tile), F32)
            for c in range(n_ctx):
                y = y + dot(act[c, i], wd[c * hidden : (c + 1) * hidden, at])
            obuf[:, ds, :, at] = y[:body].reshape(n_ctx, chunk, fold, tile).astype(BF16)
            for j in range(t * tile // cpart, (t + 1) * tile // cpart):
                lo = j * cpart - t * tile
                pick = jnp.where(gather_r == gather_c * fold + j, 1.0, 0.0).astype(BF16)
                piece = dot(pick, y[body:, lo : lo + cpart].astype(BF16))
                tail_out = piece if j == 0 else tail_out + piece
        obuf[:, ds, :, cols:] = tail_out.reshape(n_ctx, chunk, fold, cpart).astype(BF16)
        for d in order[i]:
            for m in range(n_ctx):
                if m or d:
                    ret_copy(m, d).start()
        if i == 0:
            ret[my_c, 0] = obuf[my_c, 0]

    started = [0] * n_chunks
    for kind, i, k in plan(n_k, n_chunks):
        if kind == "send":
            attend(k * fold, fold)
            dispatch(k)
        elif kind == "far":
            for d in order[-1]:
                z_copy(k, d).start()
        elif kind == "spread":
            spread(k, [d for d in order[i] if d])
        elif kind == "relay":
            relay(k, order[i])
        elif kind == "gate_up":
            gate_up(i, k, started[i] == 0, sum(started) == 0)
            started[i] += 1
            if started[i] == n_k:
                activate(i)
        else:
            down(i)

    for d in range(n_exp):
        for m in range(n_ctx):
            if m or d:
                ret_copy(m, d).wait_recv()
    lane_rank = lax.broadcasted_iota(jnp.int32, (tokens, 2 * slots), 1) % fold
    for c in range(0, n_ctx, 2):
        last = [
            ret[c + u, :, :, cols:].astype(F32).reshape(slots, cpart).astype(BF16) for u in range(2)
        ]
        last = jnp.concatenate(last, axis=1)
        for j in range(fold):
            lo = j * cpart
            main = [
                ret[c + u, :, :, lo : lo + cpart]
                .astype(F32)
                .reshape(slots, cpart)
                .astype(BF16)
                for u in range(2)
            ]
            main = jnp.concatenate(main, axis=1)
            rows = jnp.concatenate([main, main, last, last], axis=0)
            last_mix = jnp.where(lane_rank == j, mix[1].astype(F32), 0.0).astype(BF16)
            moe = dot(jnp.concatenate([mix[0], last_mix], axis=1), rows)
            for u in range(2):
                at = slice((c + u) * cols + lo, (c + u) * cols + lo + cpart)
                out_ref[:, at] = (hst[:, at] + moe[:, u * cpart : (u + 1) * cpart]).astype(BF16)

    for g in range(KV_HEADS):
        for m in range(1, n_ctx):

            @pl.when(flip(my_c, m, n_ctx) > my_c)
            def _():
                kv_copy(g, m).wait_send()

    for d in range(n_exp):
        for k in range(n_k):
            if d:
                z_copy(k, d).wait_send()
            for m in direct:
                xy_copy(m, k, d).wait_send()
            if relayed:
                relay_copy(k, d).wait_send()
        for m in range(n_ctx):
            if m or d:
                ret_copy(m, d).wait_send()
    for i in range(n_chunks):
        for m in range(1, n_ctx):
            act_copy(m, i).wait_send()


def per_device(
    n_ctx,
    n_exp,
    queries,
    keys,
    values,
    positions,
    residual,
    norm_gain,
    expert_ids,
    route_weights,
    w_gate,
    w_up,
    w_down,
):
    tokens, width = queries.shape[1:]
    inverse = yarn_frequencies()
    fold = tokens * TOP // ROUTED
    hidden = w_gate.shape[2]
    cols = w_down.shape[2]
    full = w_down.shape[1]
    n_chunks = PIECES
    rows = n_ctx * (n_exp // n_chunks) * (fold + 1)
    paired = hidden % 128 == 0
    wide = fold * HEAD_DIM
    n_k = width // wide
    spread_cols = n_k * (wide + HEAD_DIM) + HEAD_DIM
    vmem = pl.BlockSpec(memory_space=pltpu.VMEM)
    anys = pl.BlockSpec(memory_space=pl.ANY)
    dma = pltpu.SemaphoreType.DMA
    out = pl.pallas_call(
        functools.partial(kernel, n_ctx, n_exp),
        out_shape=pltpu.VMEM((tokens, width), BF16),
        in_specs=[anys] * 12,
        out_specs=vmem,
        scratch_shapes=[
            pltpu.VMEM((tokens, width), BF16),
            pltpu.VMEM((tokens, keys.shape[2]), BF16),
            pltpu.VMEM((1, tokens), jnp.int32),
            pltpu.VMEM((1, HEAD_DIM), F32),
            pltpu.VMEM((1, width), F32),
            pltpu.VMEM((TOP, tokens), jnp.int32),
            pltpu.VMEM((TOP, tokens), F32),
            pltpu.VMEM((tokens, width), BF16),
            pltpu.VMEM((n_ctx, KV_HEADS, 2, tokens, HEAD_DIM), BF16),
            pltpu.VMEM((tokens, width), F32),
            pltpu.VMEM((tokens, HEAD_DIM), F32),
            pltpu.VMEM((n_exp, fold, spread_cols), BF16),
            pltpu.VMEM((n_ctx, n_exp, fold, spread_cols), BF16),
            pltpu.VMEM((rows, wide), BF16),
            pltpu.VMEM((n_chunks, rows, 2 * hidden if paired else hidden), F32),
            pltpu.VMEM((8, 128) if paired else (n_chunks, rows, hidden), F32),
            pltpu.VMEM((n_ctx, n_chunks, rows, hidden), BF16),
            pltpu.VMEM((n_ctx, n_exp, fold, cols + cols // fold), BF16),
            pltpu.VMEM((n_ctx, n_exp, fold, cols + cols // fold), BF16),
            pltpu.VMEM((2, tokens, 2 * n_exp * fold), BF16),
            pltpu.VMEM((width, 2 * hidden if paired else hidden), BF16),
            pltpu.VMEM((16, 128) if paired else (width, hidden), BF16),
            pltpu.VMEM((full, cols), BF16),
            dma((11 + KV_HEADS,)),
            dma((KV_HEADS, n_ctx)),
            dma((KV_HEADS, n_ctx)),
            dma((n_k, n_exp)),
            dma((n_k, n_exp)),
            dma((n_ctx, n_k, n_exp)),
            dma((n_ctx, n_k, n_exp)),
            dma((n_ctx, n_chunks)),
            dma((n_ctx, n_chunks)),
            dma((n_ctx, n_exp)),
            dma((n_ctx, n_exp)),
        ],
        compiler_params=pltpu.CompilerParams(
            collective_id=0, has_side_effects=True, vmem_limit_bytes=56000 * 1024
        ),
    )(
        queries,
        keys[0],
        values[0],
        positions,
        jnp.concatenate([inverse, inverse])[None],
        residual,
        norm_gain[None],
        expert_ids[0].T,
        route_weights[0].T,
        w_gate,
        w_up,
        w_down,
    )
    return out[None]


def solution(mesh):
    return jax.shard_map(
        functools.partial(per_device, mesh.shape["ctx"], mesh.shape["exp"]),
        mesh=mesh,
        in_specs=(
            P("exp", "ctx", None),
            P("exp", "ctx", None),
            P("exp", "ctx", None),
            P("exp", "ctx"),
            P("exp", "ctx", None),
            P(),
            P("exp", "ctx", None),
            P("exp", "ctx", None),
            P("exp", None, "ctx"),
            P("exp", None, "ctx"),
            P("exp", None, "ctx"),
        ),
        out_specs=P("exp", "ctx", None),
        check_vma=False,
    )
```
